32 devices in a mesh: groups: 2 (over y), pool: 4 (over z), sub: 2 (over x), chip: 2 (over core).
Axes of the slice: x: 2, y: 2, z: 4, core: 2. Of those that a mesh axis runs over, the one named last changes fastest.
Arguments:
- hidden: bfloat16 [1024, 4096], P(('groups', 'pool', 'sub', 'chip')), parts along dimension 0, may hold values from -6 to 6
- query_weight_matrix: bfloat16 [4096, 4096], P(None, 'pool'), may hold values from -0.09375 to 0.09375
- adapter_down_weight: bfloat16 [64, 64, 4096], P('pool', None, ('sub', 'chip')), may hold values from -0.09375 to 0.09375
- adapter_up_weight: bfloat16 [64, 64, 4096], P('pool', None, ('sub', 'chip')), may hold values from -0.75 to 0.75
- adapter_index_rows: int32 [1024], P(('groups', 'pool', 'sub', 'chip')), parts along dimension 0, may hold values from 0 to 63, as said below
Outputs:
- query: bfloat16 [1024, 4096], P(('groups', 'pool', 'sub', 'chip')), parts along dimension 0
The draws below stay inside these ranges and needn't reach their ends.
There are 2 independent parts, one for each index of `groups`. The reference program is written for one: setup_inputs(seed, part) draws one part's arguments, and reference() takes and returns one part's arrays. A program takes and returns all parts, laid end to end along the dimension named above; an argument that names none is the same for every part. Nothing has to cross between parts.
Inputs may be any that keep to these rules, and one draw needn't show every extreme that they name: A row's owner is adapter_index_rows // 16. In each aligned block of 32 rows (the rows of one device) at most 12 rows have one owner, and in every block some owner has exactly 12 rows.
All inputs are finite; a program needn't handle non-finite values.
Results may differ from the reference program's by a relative error of at most 0.0052.
Values may be sent and summed in bfloat16 or wider, within the bound.
A program may use at most 64 MiB of HBM per device.

```python
import jax
import jax.numpy as jnp
from jax import lax

MODEL_WIDTH = 4096
ADAPTER_RANK = 64
ADAPT_POOL = 16
ROW_DEV = 32
OWNERS = 4
SHARDS = 4
ADAPTER_TOTAL = 64
CAP = 12
ROWS = 512


def draw_adapter_index_rows(key, part):
    blocks = ROWS // ROW_DEV
    full_count = ROW_DEV // CAP
    leftover = ROW_DEV - full_count * CAP
    group_base = jax.random.fold_in(key, 9001)

    def one_block(index):
        group_key = jax.random.fold_in(group_base, index // SHARDS)
        order = jax.random.permutation(group_key, OWNERS).astype(jnp.int32)
        full_owners = order[:full_count]
        block_key = jax.random.fold_in(key, index + 11)
        others = jax.random.permutation(jax.random.fold_in(block_key, 1), order[full_count:])
        owners = jnp.concatenate([jnp.repeat(full_owners, CAP), jnp.tile(others, CAP)[:leftover]])
        owners = jax.random.permutation(jax.random.fold_in(block_key, 2), owners)
        within = jax.random.randint(jax.random.fold_in(block_key, 3), (ROW_DEV,), 0, ADAPT_POOL)
        return owners * ADAPT_POOL + within
    return jax.vmap(one_block)(jnp.arange(blocks, dtype=jnp.int32)).reshape(ROWS).astype(jnp.int32)


def block_scale(stream_key, dims, shards, low, top_value):
    def one(position, parts):
        draws = jax.random.uniform(jax.random.fold_in(jax.random.fold_in(stream_key, 6), position), (parts,), jnp.float32, low / len(shards), top_value / len(shards))
        return jnp.repeat(jnp.exp(draws), dims[position] // parts).reshape((-1,) + (1,) * (len(dims) - position - 1))

    level = one(*shards[0])
    for cut in shards[1:]:
        level = level * one(*cut)
    return level


def centred(own_key, shape, spread, most, shards=(), kind=jnp.bfloat16):
    loudness = block_scale(own_key, shape, shards, -0.22, 0.18) if shards else 1.0
    values = jax.random.normal(own_key, shape, jnp.float32) * spread * loudness
    return jnp.minimum(jnp.maximum(values, -most), most).astype(kind)


def setup_inputs(seed: int = 0, part: int = 0) -> dict:
    key_list = jax.random.split(jax.random.key(seed), 6)
    part_splits = jax.random.split(jax.random.fold_in(key_list[5], part), 6)
    return {
        "hidden": centred(part_splits[0], (ROWS, MODEL_WIDTH), 1.0, 6.0, ((0, 16),)),
        "query_weight_matrix": centred(key_list[1], (MODEL_WIDTH, MODEL_WIDTH), MODEL_WIDTH ** -0.5, 0.09375, ((1, 4),)),
        "adapter_down_weight": centred(key_list[2], (ADAPTER_TOTAL, ADAPTER_RANK, MODEL_WIDTH), MODEL_WIDTH ** -0.5, 0.09375, ((0, 4), (2, 4))),
        "adapter_up_weight": centred(key_list[3], (ADAPTER_TOTAL, ADAPTER_RANK, MODEL_WIDTH), ADAPTER_RANK ** -0.5, 0.75, ((0, 4), (2, 4))),
        "adapter_index_rows": draw_adapter_index_rows(jax.random.fold_in(jax.random.fold_in(key_list[5], part), 71), part),
    }


ADAPTER_SCALE = 0.5


def reference(hidden, query_weight_matrix, adapter_down_weight, adapter_up_weight, adapter_index_rows):
    base = jnp.dot(hidden, query_weight_matrix, preferred_element_type=jnp.float32).astype(jnp.bfloat16)
    blocks = hidden.shape[0] // ROW_DEV
    block_rows = hidden.reshape(blocks, ROW_DEV, MODEL_WIDTH)
    block_adapters = adapter_index_rows.reshape(blocks, ROW_DEV)

    def one_block(pair):
        rows_here, resident_adapters = pair
        down_matrix = adapter_down_weight[resident_adapters].astype(jnp.float32)
        projected_down = jnp.einsum("rd,rkd->rk", rows_here.astype(jnp.float32), down_matrix).astype(jnp.bfloat16)
        projected_down = lax.optimization_barrier(projected_down).astype(jnp.float32)
        projected_up = adapter_up_weight[resident_adapters].astype(jnp.float32)
        return (ADAPTER_SCALE * jnp.einsum("fj,fjs->fs", projected_down, projected_up)).astype(jnp.bfloat16)

    update_term = lax.map(one_block, (block_rows, block_adapters)).reshape(hidden.shape[0], MODEL_WIDTH)
    base_wide = lax.optimization_barrier(base).astype(jnp.float32)
    delta_wide = lax.optimization_barrier(update_term).astype(jnp.float32)
    return (base_wide + delta_wide).astype(jnp.bfloat16)
```

```python
import functools

import jax
import jax.numpy as jnp
from jax import lax
from jax.experimental import pallas as pl
from jax.experimental.pallas import tpu as pltpu
from jax.sharding import PartitionSpec as P

ADAPTER_SCALE = 0.5
SLOTS = 16
MESH = pl.DeviceIdType.MESH
F32 = jnp.float32
BF16 = jnp.bfloat16


def tile_of(extent):
    return 256 if extent % 256 == 0 else extent


def kernel(
    pools, chips, shards, stack,
    h_ref, idx_ref, col_ref, w_hbm, dn_hbm, up_hbm, out_ref,
    x, w, dn, up, ids, picked, rows, low_out, low, delta, home_delta, base, home_base, acc,
    wsem, isend, irecv, hright, hleft, hrecv, rsend, rrecv, lsend, lrecv, bsend, brecv, dsend, drecv,
):
    p = lax.axis_index("pool")
    me = lax.axis_index("sub") * chips + lax.axis_index("chip")
    rows_dev, width = h_ref.shape
    cols = w.shape[1]
    part = width // shards
    half = width // 2
    ranks = dn.shape[0] // stack
    many = shards * SLOTS

    def rcopy(src, dst, ssem, rsem, z, sh):
        return pltpu.make_async_remote_copy(
            src_ref=src, dst_ref=dst, send_sem=ssem, recv_sem=rsem,
            device_id={"pool": z, "sub": sh // chips, "chip": sh % chips},
            device_id_type=MESH,
        )

    def others(f):
        def step(z, carry):
            for sh in range(shards):
                @pl.when(jnp.logical_or(z != p, sh != me))
                def _():
                    f(z, sh)
            return carry
        lax.fori_loop(0, pools, step, 0)

    loads = [
        pltpu.make_async_copy(w_hbm.at[pl.ds(0, half)], w.at[pl.ds(0, half)], wsem.at[0]),
        pltpu.make_async_copy(w_hbm.at[pl.ds(half, half)], w.at[pl.ds(half, half)], wsem.at[1]),
        pltpu.make_async_copy(dn_hbm, dn, wsem.at[2]),
        pltpu.make_async_copy(up_hbm, up, wsem.at[3]),
    ]
    for load in (loads[2], loads[0], loads[3], loads[1]):
        load.start()

    barrier = pltpu.get_barrier_semaphore()

    def greet(z, sh):
        pl.semaphore_signal(
            barrier, inc=1,
            device_id={"pool": z, "sub": sh // chips, "chip": sh % chips}, device_id_type=MESH,
        )

    others(greet)
    pl.semaphore_wait(barrier, pools * shards - 1)

    mine = p * shards + me

    def id_copy(z, sh):
        return rcopy(idx_ref, ids.at[mine], isend.at[z * shards + sh], irecv.at[mine], z, sh)

    others(lambda z, sh: id_copy(z, sh).start())

    def piece(q):
        return pl.ds(q * part, part)

    def to_right(src, b, q):
        return rcopy(src, x.at[b, :, piece(q)], hright.at[b, q], hrecv.at[b, q], p + 1, me)

    def to_left(src, b, q):
        return rcopy(src, x.at[b, :, piece(q)], hleft.at[b, q], hrecv.at[b, q], p - 1, me)

    for q in range(shards):
        @pl.when(p + 1 < pools)
        def _():
            to_right(h_ref.at[:, piece(q)], p, q).start()

        @pl.when(p >= 1)
        def _():
            to_left(h_ref.at[:, piece(q)], p, q).start()

    x[p] = h_ref[...]
    ids[mine] = idx_ref[...]

    def id_wait(z, sh):
        g = z * shards + sh
        rcopy(idx_ref, ids.at[g], isend.at[g], irecv.at[g], z, sh).wait_recv()

    others(id_wait)

    def selection(g):
        number = jnp.broadcast_to(ids[g][:, :rows_dev], (SLOTS, rows_dev)) - p * stack
        owned = jnp.logical_and(number >= 0, number < stack)
        before = (
            lax.broadcasted_iota(jnp.int32, (rows_dev, rows_dev), 0)
            < lax.broadcasted_iota(jnp.int32, (rows_dev, rows_dev), 1)
        )
        rank = jnp.dot(
            jnp.where(owned, 1.0, 0.0).astype(BF16), jnp.where(before, 1.0, 0.0).astype(BF16),
            preferred_element_type=F32,
        )
        slot = lax.broadcasted_iota(jnp.int32, (SLOTS, rows_dev), 0).astype(F32)
        hit = jnp.logical_and(owned, rank == slot)
        return jnp.where(hit, 1.0, 0.0), number.astype(F32)

    def pick(b, chosen, q):
        got = jnp.dot(chosen, x[b, :, piece(q)], preferred_element_type=F32).astype(BF16)

        @pl.when(q != me)
        def _():
            picked[b, q] = got
            rcopy(picked.at[b, q], rows.at[b, me], rsend.at[b, q], rrecv.at[b, me], p, q).start()

        @pl.when(q == me)
        def _():
            rows[b, me] = got

    def receive(b, from_left):
        chosen = selection(b * shards + me)[0].astype(BF16)
        for q in range(shards):
            dst = x.at[b, :, piece(q)]
            rcopy(dst, dst, hright.at[b, q], hrecv.at[b, q], p, (me + 1) % shards).wait_recv()
            if from_left:
                @pl.when(p + 1 < pools)
                def _():
                    to_right(x.at[b, :, piece(q)], b, q).start()
            else:
                @pl.when(p >= 1)
                def _():
                    to_left(x.at[b, :, piece(q)], b, q).start()
            pick(b, chosen, q)

    def peers():
        return [(me + d) % shards for d in range(1, shards)]

    def project(b, k, last):
        tile = tile_of(cols)

        def step(j, carry):
            at = pl.ds(pl.multiple_of(j * tile, tile), tile)
            term = jnp.dot(
                x[b, :, pl.ds(k * half, half)], w[pl.ds(k * half, half), at],
                preferred_element_type=F32,
            )
            if last:
                base[b, :, at] = (acc[:, at] + term).astype(BF16)
            else:
                acc[:, at] = term
            return carry

        lax.fori_loop(0, cols // tile, step, 0)

    mine_cols = pl.ds(pl.multiple_of(p * cols, 128), cols)

    def base_copy(b):
        return rcopy(base.at[b], home_base.at[:, mine_cols], bsend.at[b], brecv.at[p], b, me)

    def delta_copy(b, sh):
        return rcopy(
            delta.at[b, sh], home_delta.at[me, pl.ds(pl.multiple_of(p * SLOTS, SLOTS), SLOTS)],
            dsend.at[b, sh], drecv.at[p, me], b, sh,
        )

    def process(b, own):
        if own:
            loads[0].wait()
        project(b, 0, False)

        parts = []
        for sh in range(shards):
            hit, number = selection(b * shards + sh)
            parts.append(jnp.sum(hit * number, axis=1, keepdims=True))
        adapter = jnp.concatenate(parts, axis=0).astype(jnp.int32)

        for sh in peers():
            rcopy(rows.at[b, sh], rows.at[b, sh], rsend.at[b, sh], rrecv.at[b, sh], p, sh).wait_recv()
        if own:
            loads[2].wait()
        here = rows[b].reshape(many, part)
        lane = lax.broadcasted_iota(jnp.int32, (many, 256), 1) // ranks
        each = 256 // ranks
        total = jnp.zeros((many, 128), F32)
        for j in range(stack * ranks // 256):
            term = lax.dot_general(
                here, dn[pl.ds(j * 256, 256), :], (((1,), (1,)), ((), ())),
                preferred_element_type=F32,
            )
            term = jnp.where(lane + j * each == adapter, term, 0.0)
            total = total + term[:, :128] + term[:, 128:]
        total = total + pltpu.roll(total, 64, 1)
        lower = lax.broadcasted_iota(jnp.int32, (many // 2, 128), 1) < 64
        packed = jnp.where(lower, total[: many // 2], total[many // 2 :])
        low_out[b] = packed
        low[b, me] = packed
        for sh in peers():
            rcopy(low_out.at[b], low.at[b, me], lsend.at[b, sh], lrecv.at[b, me], p, sh).start()

        if own:
            loads[1].wait()
        project(b, 1, True)
        if own:
            home_base[:, mine_cols] = base[b]
        else:
            base_copy(b).start()

        for sh in peers():
            rcopy(low_out.at[b], low.at[b, sh], lsend.at[b, sh], lrecv.at[b, sh], p, sh).wait_recv()
        both = low[b, 0]
        for sh in range(1, shards):
            both = both + low[b, sh]
        both = both.astype(BF16).astype(F32)
        turned = pltpu.roll(both, 64, 1)
        full = jnp.concatenate(
            [jnp.where(lower, both, turned), jnp.where(lower, turned, both)], axis=0
        )
        full = jnp.concatenate([full, full], axis=1)
        spread = jnp.concatenate(
            [
                jnp.where(lane + j * each == adapter, full, 0.0).astype(BF16)
                for j in range(stack * ranks // 256)
            ],
            axis=1,
        )
        if own:
            loads[3].wait()
        for j in range(part // 256):
            at = pl.ds(j * 256, 256)
            term = jnp.dot(spread, up[:, at], preferred_element_type=F32)
            delta[b, :, :, at] = (ADAPTER_SCALE * term).astype(BF16).reshape(shards, SLOTS, 256)
        for sh in range(shards):
            if own:
                @pl.when(sh != me)
                def _():
                    delta_copy(b, sh).start()

                @pl.when(sh == me)
                def _():
                    home_delta[me, pl.ds(pl.multiple_of(p * SLOTS, SLOTS), SLOTS)] = delta[b, sh]
            else:
                delta_copy(b, sh).start()

    chosen_here = selection(mine)[0].astype(BF16)
    for q in range(shards):
        pick(p, chosen_here, q)
    process(p, True)

    def receive_step(t):
        @pl.when(p - 1 - t >= 0)
        def _():
            receive(p - 1 - t, True)

        @pl.when(p + 1 + t < pools)
        def _():
            receive(p + 1 + t, False)

    receive_step(0)

    def step(t, carry):
        left = p - 1 - t >= 0
        right = p + 1 + t < pools

        def turn(i, c):
            b = jnp.where(i == 0, p - 1 - t, p + 1 + t)

            @pl.when(jnp.logical_and(b >= 0, b < pools))
            def _():
                process(b, False)

            @pl.when(i == jnp.where(jnp.logical_and(left, right), 0, 1))
            def _():
                receive_step(t + 1)
            return c

        return lax.fori_loop(0, 2, turn, carry)

    lax.fori_loop(0, pools - 1, step, 0)

    column = col_ref[...]
    slots = pools * SLOTS
    lanes = lax.broadcasted_iota(jnp.int32, (rows_dev, slots), 1)
    owner = jnp.where(column // stack == lanes // SLOTS, 1.0, 0.0)
    after = (
        lax.broadcasted_iota(jnp.int32, (rows_dev, rows_dev), 0)
        > lax.broadcasted_iota(jnp.int32, (rows_dev, rows_dev), 1)
    )
    rank = jnp.dot(
        jnp.where(after, 1.0, 0.0).astype(BF16), owner.astype(BF16), preferred_element_type=F32
    )
    place = jnp.where(rank == (lanes % SLOTS).astype(F32), owner, 0.0).astype(BF16)

    def base_wait(z, carry):
        @pl.when(z != p)
        def _():
            dst = home_base.at[:, pl.ds(pl.multiple_of(z * cols, 128), cols)]
            rcopy(base.at[z], dst, bsend.at[z], brecv.at[z], z, me).wait_recv()
        return carry

    lax.fori_loop(0, pools, base_wait, 0)

    def delta_wait(z, sh):
        dst = home_delta.at[sh, pl.ds(pl.multiple_of(z * SLOTS, SLOTS), SLOTS)]
        rcopy(delta.at[z, sh], dst, dsend.at[z, sh], drecv.at[z, sh], z, sh).wait_recv()

    others(delta_wait)
    for sh in range(shards):
        term = jnp.dot(place, home_delta[sh], preferred_element_type=F32)
        out_ref[:, piece(sh)] = (home_base[:, piece(sh)].astype(F32) + term).astype(BF16)

    others(lambda z, sh: id_copy(z, sh).wait_send())
    others(lambda z, sh: delta_copy(z, sh).wait_send())

    def drain(b, carry):
        for q in range(shards):
            @pl.when(jnp.logical_and(b <= p, p + 1 < pools))
            def _():
                to_right(x.at[b, :, piece(q)], b, q).wait_send()

            @pl.when(jnp.logical_and(b >= p, p >= 1))
            def _():
                to_left(x.at[b, :, piece(q)], b, q).wait_send()

            @pl.when(q != me)
            def _():
                rcopy(picked.at[b, q], rows.at[b, me], rsend.at[b, q], rrecv.at[b, me], p, q).wait_send()
                rcopy(low_out.at[b], low.at[b, me], lsend.at[b, q], lrecv.at[b, me], p, q).wait_send()

        @pl.when(b != p)
        def _():
            base_copy(b).wait_send()
        return carry

    lax.fori_loop(0, pools, drain, 0)


def local(hidden, query_weight_matrix, adapter_down_weight, adapter_up_weight, adapter_index_rows):
    pools = lax.axis_size("pool")
    chips = lax.axis_size("chip")
    shards = lax.axis_size("sub") * chips
    row_count, width = hidden.shape
    cols = query_weight_matrix.shape[1]
    stack, ranks, part = adapter_down_weight.shape
    dma = pltpu.SemaphoreType.DMA
    vmem = pl.BlockSpec(memory_space=pltpu.VMEM)
    hbm = pl.BlockSpec(memory_space=pl.ANY)
    index_line = jnp.pad(adapter_index_rows[None, :], ((0, 0), (0, 128 - row_count)))
    return pl.pallas_call(
        functools.partial(kernel, pools, chips, shards, stack),
        out_shape=jax.ShapeDtypeStruct((row_count, width), BF16),
        in_specs=[vmem, vmem, vmem, hbm, hbm, hbm],
        out_specs=vmem,
        scratch_shapes=[
            pltpu.VMEM((pools, row_count, width), BF16),
            pltpu.VMEM((width, cols), BF16),
            pltpu.VMEM((stack * ranks, part), BF16),
            pltpu.VMEM((stack * ranks, part), BF16),
            pltpu.VMEM((pools * shards, 1, 128), jnp.int32),
            pltpu.VMEM((pools, shards, SLOTS, part), BF16),
            pltpu.VMEM((pools, shards, SLOTS, part), BF16),
            pltpu.VMEM((pools, shards * SLOTS // 2, 128), F32),
            pltpu.VMEM((pools, shards, shards * SLOTS // 2, 128), F32),
            pltpu.VMEM((pools, shards, SLOTS, part), BF16),
            pltpu.VMEM((shards, pools * SLOTS, part), BF16),
            pltpu.VMEM((pools, row_count, cols), BF16),
            pltpu.VMEM((row_count, width), BF16),
            pltpu.VMEM((row_count, cols), F32),
            dma((4,)),
            dma((pools * shards,)),
            dma((pools * shards,)),
            dma((pools, shards)),
            dma((pools, shards)),
            dma((pools, shards)),
            dma((pools, shards)),
            dma((pools, shards)),
            dma((pools, shards)),
            dma((pools, shards)),
            dma((pools,)),
            dma((pools,)),
            dma((pools, shards)),
            dma((pools, shards)),
        ],
        compiler_params=pltpu.CompilerParams(
            collective_id=0, has_side_effects=True, vmem_limit_bytes=56 * 1024 * 1024
        ),
    )(
        hidden,
        index_line,
        adapter_index_rows[:, None],
        query_weight_matrix,
        adapter_down_weight.reshape(stack * ranks, part),
        adapter_up_weight.reshape(stack * ranks, part),
    )


def solution(mesh):
    in_specs = (
        P(("groups", "pool", "sub", "chip"), None),
        P(None, "pool"),
        P("pool", None, ("sub", "chip")),
        P("pool", None, ("sub", "chip")),
        P(("groups", "pool", "sub", "chip")),
    )
    out_specs = P(("groups", "pool", "sub", "chip"), None)
    return jax.shard_map(local, mesh=mesh, in_specs=in_specs, out_specs=out_specs, check_vma=False)
```

```python
import functools

import jax
import jax.numpy as jnp
from jax import lax
from jax.experimental import pallas as pl
from jax.experimental.pallas import tpu as pltpu
from jax.sharding import PartitionSpec as P

ADAPTER_SCALE = 0.5
SLOTS = 16
HELD = 12
META = 128
MESH = pl.DeviceIdType.MESH
F32 = jnp.float32
BF16 = jnp.bfloat16


def tile_of(extent):
    return 256 if extent % 256 == 0 else extent


def kernel(
    pools, chips, shards, stack,
    h_hbm, idx_ref, w_hbm, dn_hbm, up_hbm, out_ref,
    x, w, dn, up, picked, rows, low_out, low, delta, home_delta, base, home_base, acc,
    wsem, hright, hleft, hrecv, rsend, rrecv, lsend, lrecv, bsend, brecv, dsend, drecv,
):
    p = lax.axis_index("pool")
    me = lax.axis_index("sub") * chips + lax.axis_index("chip")
    rows_dev, width = h_hbm.shape
    cols = w.shape[1]
    part = width // shards
    half = width // 2
    quarter = part // 4
    ranks = dn.shape[0] // stack
    tiles = stack * ranks // 256
    each = 256 // ranks
    many = shards * SLOTS

    def where_is(z, sh):
        return {"pool": z, "sub": sh // chips, "chip": sh % chips}

    def rcopy(src, dst, ssem, rsem, z, sh):
        return pltpu.make_async_remote_copy(
            src_ref=src, dst_ref=dst, send_sem=ssem, recv_sem=rsem,
            device_id=where_is(z, sh), device_id_type=MESH,
        )

    peers = [(me + d) % shards for d in range(1, shards)]

    barrier = pltpu.get_barrier_semaphore()

    def greet(z, sh):
        pl.semaphore_signal(barrier, inc=1, device_id=where_is(z, sh), device_id_type=MESH)

    @pl.when(p >= 1)
    def _():
        greet(p - 1, me)

    @pl.when(p + 1 < pools)
    def _():
        greet(p + 1, me)

    for sh in peers:
        greet(p, sh)

    loads = [
        pltpu.make_async_copy(w_hbm.at[pl.ds(0, half)], w.at[pl.ds(0, half)], wsem.at[0]),
        pltpu.make_async_copy(w_hbm.at[pl.ds(half, half)], w.at[pl.ds(half, half)], wsem.at[1]),
        pltpu.make_async_copy(dn_hbm, dn, wsem.at[2]),
        pltpu.make_async_copy(up_hbm, up, wsem.at[3]),
        pltpu.make_async_copy(h_hbm, x.at[p, :, pl.ds(META, width)], wsem.at[4]),
    ]
    for i in (4, 0, 2, 1, 3):
        loads[i].start()

    square = (rows_dev, rows_dev)
    down_axis = lax.broadcasted_iota(jnp.int32, square, 0)
    along = lax.broadcasted_iota(jnp.int32, square, 1)
    index = jnp.broadcast_to(idx_ref[...], square).astype(F32)
    column = jnp.sum(jnp.where(down_axis == along, index, 0.0), axis=1, keepdims=True)
    column = column.astype(jnp.int32)
    owner_column = column // stack
    first = lax.broadcasted_iota(jnp.int32, (rows_dev, META), 1) == 0
    meta = jnp.where(first, owner_column, column - owner_column * stack)
    x[p, :, pl.ds(0, META)] = meta.astype(F32).astype(BF16)

    greeters = jnp.minimum(p, 1) + jnp.minimum(pools - 1 - p, 1) + shards - 1
    pl.semaphore_wait(barrier, greeters)
    loads[4].wait()

    def piece(q):
        return pl.ds(META + q * part, part)

    def sent(q):
        return pl.ds(0, META + part) if q == 0 else piece(q)

    def to_right(b, q):
        ref = x.at[b, :, sent(q)]
        return rcopy(ref, ref, hright.at[b, q], hrecv.at[b, q], p + 1, me)

    def to_left(b, q):
        ref = x.at[b, :, sent(q)]
        return rcopy(ref, ref, hleft.at[b, q], hrecv.at[b, q], p - 1, me)

    for q in range(shards):
        @pl.when(p + 1 < pools)
        def _():
            to_right(p, q).start()

        @pl.when(p >= 1)
        def _():
            to_left(p, q).start()

    before = jnp.where(down_axis < along, 1.0, 0.0).astype(BF16)

    def selection(b):
        pick_owner = lax.broadcasted_iota(jnp.int32, (SLOTS, META), 1) == 0
        owner = lax.dot_general(
            jnp.where(pick_owner, 1.0, 0.0).astype(BF16), x[b, :, pl.ds(0, META)],
            (((1,), (1,)), ((), ())), preferred_element_type=F32,
        )
        owned = jnp.where(owner == p.astype(F32), 1.0, 0.0)
        rank = jnp.dot(owned.astype(BF16), before, preferred_element_type=F32)
        slot = lax.broadcasted_iota(jnp.int32, (SLOTS, rows_dev), 0).astype(F32)
        return jnp.where(rank == slot, owned, 0.0).astype(BF16)

    def pick(b, chosen, tag, q):
        got = jnp.dot(chosen, x[b, :, piece(q)], preferred_element_type=F32).astype(BF16)

        @pl.when(q != me)
        def _():
            picked[b, q, :, pl.ds(0, META)] = tag
            picked[b, q, :, pl.ds(META, part)] = got
            rcopy(picked.at[b, q], rows.at[b, me], rsend.at[b, q], rrecv.at[b, me], p, q).start()

        @pl.when(q == me)
        def _():
            rows[b, me, :, pl.ds(0, META)] = tag
            rows[b, me, :, pl.ds(META, part)] = got

    def select_tag(b):
        chosen = selection(b)
        tag = jnp.dot(chosen, x[b, :, pl.ds(0, META)], preferred_element_type=F32).astype(BF16)
        return chosen, tag

    def arrive(b, q, from_left):
        rcopy(
            x.at[b, :, sent(q)], x.at[b, :, sent(q)], hright.at[b, q], hrecv.at[b, q], p, peers[0]
        ).wait_recv()
        if from_left:
            @pl.when(p + 1 < pools)
            def _():
                to_right(b, q).start()
        else:
            @pl.when(p >= 1)
            def _():
                to_left(b, q).start()

    def receive(b, from_left):
        arrive(b, 0, from_left)
        chosen, tag = select_tag(b)
        pick(b, chosen, tag, 0)
        for q in range(1, shards):
            arrive(b, q, from_left)
            pick(b, chosen, tag, q)

    def project(b, k, last):
        tile = tile_of(cols)

        def step(j, carry):
            at = pl.ds(pl.multiple_of(j * tile, tile), tile)
            term = jnp.dot(
                x[b, :, pl.ds(META + k * half, half)], w[pl.ds(k * half, half), at],
                preferred_element_type=F32,
            )
            if last:
                base[b, :, at] = (acc[b, :, at] + term).astype(BF16)
            else:
                acc[b, :, at] = term
            return carry

        lax.fori_loop(0, cols // tile, step, 0)

    mine_cols = pl.ds(pl.multiple_of(p * cols, 128), cols)
    mine_slots = pl.ds(pl.multiple_of(p * SLOTS, SLOTS), SLOTS)

    def base_copy(b):
        return rcopy(base.at[b], home_base.at[:, mine_cols], bsend.at[b], brecv.at[p], b, me)

    def delta_copy(b, sh):
        return rcopy(
            delta.at[b, sh], home_delta.at[me, mine_slots], dsend.at[b, sh], drecv.at[p, me], b, sh
        )

    lane = lax.broadcasted_iota(jnp.int32, (many, 256), 1) // ranks
    lower = lax.broadcasted_iota(jnp.int32, (many // 2, 128), 1) < 64

    def adapter_of(b):
        tag = rows[b, :, :, pl.ds(0, META)].reshape(many, META).astype(F32)
        return tag[:, 1:2].astype(jnp.int32)

    def shrink(b):
        for sh in peers:
            rcopy(rows.at[b, sh], rows.at[b, sh], rsend.at[b, sh], rrecv.at[b, sh], p, sh).wait_recv()
        adapter = adapter_of(b)
        here = rows[b, :, :, pl.ds(META, part)].reshape(many, part)
        total = jnp.zeros((many, 128), F32)
        for j in range(tiles):
            term = lax.dot_general(
                here, dn[pl.ds(j * 256, 256), :], (((1,), (1,)), ((), ())),
                preferred_element_type=F32,
            )
            term = jnp.where(lane + j * each == adapter, term, 0.0)
            total = total + term[:, :128] + term[:, 128:]
        total = total + pltpu.roll(total, 64, 1)
        packed = jnp.where(lower, total[: many // 2], total[many // 2 :])
        low_out[b] = packed
        low[b, me] = packed
        for sh in peers:
            rcopy(low_out.at[b], low.at[b, me], lsend.at[b, sh], lrecv.at[b, me], p, sh).start()

    def grow(b):
        for sh in peers:
            rcopy(low_out.at[b], low.at[b, sh], lsend.at[b, sh], lrecv.at[b, sh], p, sh).wait_recv()
        adapter = adapter_of(b)
        both = low[b, 0]
        for sh in range(1, shards):
            both = both + low[b, sh]
        both = both.astype(BF16).astype(F32)
        turned = pltpu.roll(both, 64, 1)
        full = jnp.concatenate(
            [jnp.where(lower, both, turned), jnp.where(lower, turned, both)], axis=0
        )
        full = jnp.concatenate([full, full], axis=1)
        spread = jnp.concatenate(
            [
                jnp.where(lane + j * each == adapter, full, 0.0).astype(BF16)
                for j in range(tiles)
            ],
            axis=1,
        )
        rest = jnp.dot(spread, up[:, pl.ds(3 * quarter, quarter)], preferred_element_type=F32)
        top = lax.broadcasted_iota(jnp.int32, (many, quarter), 0) % SLOTS < HELD
        for j in range(3):
            at = pl.ds(j * quarter, quarter)
            term = jnp.dot(spread, up[:, at], preferred_element_type=F32)
            term = jnp.where(top, term, pltpu.roll(rest, HELD - 4 * j, 0))
            delta[b, :, :, at] = (ADAPTER_SCALE * term).astype(BF16).reshape(shards, SLOTS, quarter)
        for sh in range(shards):
            @pl.when(jnp.logical_or(b != p, sh != me))
            def _():
                delta_copy(b, sh).start()

            @pl.when(jnp.logical_and(b == p, sh == me))
            def _():
                home_delta[me, mine_slots] = delta[b, sh]

    def both_sides(t, f):
        def turn(i, c):
            b = jnp.where(i == 0, p - t, p + t)
            valid = jnp.logical_and(jnp.logical_and(b >= 0, b < pools), jnp.logical_or(i == 0, t > 0))

            @pl.when(valid)
            def _():
                f(b)
            return c

        lax.fori_loop(0, 2, turn, 0)

    chosen, tag = select_tag(p)
    for q in range(shards):
        pick(p, chosen, tag, q)

    def step(t, carry):
        @pl.when(t == 0)
        def _():
            loads[0].wait()
        both_sides(t, lambda b: project(b, 0, False))

        @pl.when(t == 0)
        def _():
            loads[2].wait()
        both_sides(t, shrink)

        @pl.when(t == 0)
        def _():
            loads[1].wait()

        def finish(b):
            project(b, 1, True)

            @pl.when(b != p)
            def _():
                base_copy(b).start()

            @pl.when(b == p)
            def _():
                home_base[:, mine_cols] = base[b]

        both_sides(t, finish)

        @pl.when(p - 1 - t >= 0)
        def _():
            receive(p - 1 - t, True)

        @pl.when(p + 1 + t < pools)
        def _():
            receive(p + 1 + t, False)

        @pl.when(t == 0)
        def _():
            loads[3].wait()
        both_sides(t, grow)
        return carry

    lax.fori_loop(0, pools, step, 0)

    slots = pools * SLOTS
    lanes = lax.broadcasted_iota(jnp.int32, (rows_dev, slots), 1)
    owner = jnp.where(owner_column == lanes // SLOTS, 1.0, 0.0)
    after = jnp.where(down_axis > along, 1.0, 0.0).astype(BF16)
    rank = jnp.dot(after, owner.astype(BF16), preferred_element_type=F32)
    seat = lanes % SLOTS
    place = jnp.where(rank == seat.astype(F32), owner, 0.0).astype(BF16)
    tails = [
        jnp.where(
            jnp.logical_and(seat >= HELD, rank == (seat - HELD + 4 * k).astype(F32)), owner, 0.0
        ).astype(BF16)
        for k in range(3)
    ]

    def base_wait(z, carry):
        @pl.when(z != p)
        def _():
            dst = home_base.at[:, pl.ds(pl.multiple_of(z * cols, 128), cols)]
            rcopy(base.at[z], dst, bsend.at[z], brecv.at[z], z, me).wait_recv()
        return carry

    lax.fori_loop(0, pools, base_wait, 0)

    for sh in range(shards):
        def delta_wait(z, carry):
            @pl.when(jnp.logical_or(z != p, sh != me))
            def _():
                dst = home_delta.at[sh, pl.ds(pl.multiple_of(z * SLOTS, SLOTS), SLOTS)]
                rcopy(delta.at[z, sh], dst, dsend.at[z, sh], drecv.at[z, sh], z, sh).wait_recv()
            return carry

        lax.fori_loop(0, pools, delta_wait, 0)
        start = sh * part
        wide = 3 * quarter
        term = jnp.dot(place, home_delta[sh], preferred_element_type=F32)
        at = pl.ds(start, wide)
        out_ref[:, at] = (home_base[:, at].astype(F32) + term).astype(BF16)
        term = jnp.zeros((rows_dev, quarter), F32)
        for k in range(3):
            term = term + jnp.dot(
                tails[k], home_delta[sh, :, pl.ds(k * quarter, quarter)], preferred_element_type=F32
            )
        at = pl.ds(start + wide, quarter)
        out_ref[:, at] = (home_base[:, at].astype(F32) + term).astype(BF16)

    def drain(b, carry):
        for q in range(shards):
            @pl.when(jnp.logical_and(b <= p, p + 1 < pools))
            def _():
                to_right(b, q).wait_send()

            @pl.when(jnp.logical_and(b >= p, p >= 1))
            def _():
                to_left(b, q).wait_send()

            @pl.when(q != me)
            def _():
                rcopy(picked.at[b, q], rows.at[b, me], rsend.at[b, q], rrecv.at[b, me], p, q).wait_send()
                rcopy(low_out.at[b], low.at[b, me], lsend.at[b, q], lrecv.at[b, me], p, q).wait_send()

            @pl.when(jnp.logical_or(b != p, q != me))
            def _():
                delta_copy(b, q).wait_send()

        @pl.when(b != p)
        def _():
            base_copy(b).wait_send()
        return carry

    lax.fori_loop(0, pools, drain, 0)


def local(hidden, query_weight_matrix, adapter_down_weight, adapter_up_weight, adapter_index_rows):
    pools = lax.axis_size("pool")
    chips = lax.axis_size("chip")
    shards = lax.axis_size("sub") * chips
    row_count, width = hidden.shape
    cols = query_weight_matrix.shape[1]
    stack, ranks, part = adapter_down_weight.shape
    if 2 + row_count // (pools - 1) > HELD:
        raise ValueError("owner overflow")
    dma = pltpu.SemaphoreType.DMA
    vmem = pl.BlockSpec(memory_space=pltpu.VMEM)
    hbm = pl.BlockSpec(memory_space=pl.ANY)
    return pl.pallas_call(
        functools.partial(kernel, pools, chips, shards, stack),
        out_shape=jax.ShapeDtypeStruct((row_count, width), BF16),
        in_specs=[hbm, vmem, hbm, hbm, hbm],
        out_specs=vmem,
        scratch_shapes=[
            pltpu.VMEM((pools, row_count, META + width), BF16),
            pltpu.VMEM((width, cols), BF16),
            pltpu.VMEM((stack * ranks, part), BF16),
            pltpu.VMEM((stack * ranks, part), BF16),
            pltpu.VMEM((pools, shards, SLOTS, META + part), BF16),
            pltpu.VMEM((pools, shards, SLOTS, META + part), BF16),
            pltpu.VMEM((pools, shards * SLOTS // 2, 128), F32),
            pltpu.VMEM((pools, shards, shards * SLOTS // 2, 128), F32),
            pltpu.VMEM((pools, shards, SLOTS, part - part // 4), BF16),
            pltpu.VMEM((shards, pools * SLOTS, part - part // 4), BF16),
            pltpu.VMEM((pools, row_count, cols), BF16),
            pltpu.VMEM((row_count, width), BF16),
            pltpu.VMEM((pools, row_count, cols), F32),
            dma((5,)),
            dma((pools, shards)),
            dma((pools, shards)),
            dma((pools, shards)),
            dma((pools, shards)),
            dma((pools, shards)),
            dma((pools, shards)),
            dma((pools, shards)),
            dma((pools,)),
            dma((pools,)),
            dma((pools, shards)),
            dma((pools, shards)),
        ],
        compiler_params=pltpu.CompilerParams(
            collective_id=0, has_side_effects=True, vmem_limit_bytes=56 * 1024 * 1024
        ),
    )(
        hidden,
        adapter_index_rows[None, :],
        query_weight_matrix,
        adapter_down_weight.reshape(stack * ranks, part),
        adapter_up_weight.reshape(stack * ranks, part),
    )


def solution(mesh):
    in_specs = (
        P(("groups", "pool", "sub", "chip"), None),
        P(None, "pool"),
        P("pool", None, ("sub", "chip")),
        P("pool", None, ("sub", "chip")),
        P(("groups", "pool", "sub", "chip")),
    )
    out_specs = P(("groups", "pool", "sub", "chip"), None)
    return jax.shard_map(local, mesh=mesh, in_specs=in_specs, out_specs=out_specs, check_vma=False)
```

```python
import functools

import jax
import jax.numpy as jnp
from jax import lax
from jax.experimental import pallas as pl
from jax.experimental.pallas import tpu as pltpu
from jax.sharding import PartitionSpec as P

ADAPTER_SCALE = 0.5
SLOTS = 16
HELD = 12
META = 128
MESH = pl.DeviceIdType.MESH
F32 = jnp.float32
BF16 = jnp.bfloat16


def tile_of(extent):
    return 256 if extent % 256 == 0 else extent


def kernel(
    pools, chips, shards, stack,
    h_hbm, idx_ref, w_hbm, dn_hbm, up_hbm, out_ref,
    x, w, dn, up, chosen, tags, picked, rows, low_out, low, delta, home_delta, base, home_base, acc,
    wsem, hright, hleft, hrecv, rsend, rrecv, lsend, lrecv, bsend, brecv, dsend, drecv,
):
    p = lax.axis_index("pool")
    me = lax.axis_index("sub") * chips + lax.axis_index("chip")
    rows_dev, width = h_hbm.shape
    cols = w.shape[1]
    part = width // shards
    half = width // 2
    quarter = part // 4
    ranks = dn.shape[0] // stack
    tiles = stack * ranks // 256
    each = 256 // ranks
    many = shards * SLOTS

    def where_is(z, sh):
        return {"pool": z, "sub": sh // chips, "chip": sh % chips}

    def rcopy(src, dst, ssem, rsem, z, sh):
        return pltpu.make_async_remote_copy(
            src_ref=src, dst_ref=dst, send_sem=ssem, recv_sem=rsem,
            device_id=where_is(z, sh), device_id_type=MESH,
        )

    peers = [(me + d) % shards for d in range(1, shards)]

    barrier = pltpu.get_barrier_semaphore()

    def greet(z, sh):
        pl.semaphore_signal(barrier, inc=1, device_id=where_is(z, sh), device_id_type=MESH)

    @pl.when(p >= 1)
    def _():
        greet(p - 1, me)

    @pl.when(p + 1 < pools)
    def _():
        greet(p + 1, me)

    for sh in peers:
        greet(p, sh)

    loads = [
        pltpu.make_async_copy(w_hbm.at[pl.ds(0, half)], w.at[pl.ds(0, half)], wsem.at[0]),
        pltpu.make_async_copy(w_hbm.at[pl.ds(half, half)], w.at[pl.ds(half, half)], wsem.at[1]),
        pltpu.make_async_copy(dn_hbm, dn, wsem.at[2]),
        pltpu.make_async_copy(up_hbm, up, wsem.at[3]),
        pltpu.make_async_copy(h_hbm, x.at[p, :, pl.ds(META, width)], wsem.at[4]),
    ]
    for i in (4, 0, 2, 1, 3):
        loads[i].start()

    square = (rows_dev, rows_dev)
    down_axis = lax.broadcasted_iota(jnp.int32, square, 0)
    along = lax.broadcasted_iota(jnp.int32, square, 1)
    index = jnp.broadcast_to(idx_ref[...], square).astype(F32)
    column = jnp.sum(jnp.where(down_axis == along, index, 0.0), axis=1, keepdims=True)
    column = column.astype(jnp.int32)
    owner_column = column // stack
    first = lax.broadcasted_iota(jnp.int32, (rows_dev, META), 1) == 0
    meta = jnp.where(first, owner_column, column - owner_column * stack)
    x[p, :, pl.ds(0, META)] = meta.astype(F32).astype(BF16)

    greeters = jnp.minimum(p, 1) + jnp.minimum(pools - 1 - p, 1) + shards - 1
    pl.semaphore_wait(barrier, greeters)
    loads[4].wait()

    def piece(q):
        return pl.ds(META + q * part, part)

    def sent(q):
        return pl.ds(0, META + part) if q == 0 else piece(q)

    def to_right(b, q):
        ref = x.at[b, :, sent(q)]
        return rcopy(ref, ref, hright.at[b, q], hrecv.at[b, q], p + 1, me)

    def to_left(b, q):
        ref = x.at[b, :, sent(q)]
        return rcopy(ref, ref, hleft.at[b, q], hrecv.at[b, q], p - 1, me)

    for q in range(shards):
        @pl.when(p + 1 < pools)
        def _():
            to_right(p, q).start()

        @pl.when(p >= 1)
        def _():
            to_left(p, q).start()

    before = jnp.where(down_axis < along, 1.0, 0.0).astype(BF16)

    def selection(b):
        pick_owner = lax.broadcasted_iota(jnp.int32, (SLOTS, META), 1) == 0
        owner = lax.dot_general(
            jnp.where(pick_owner, 1.0, 0.0).astype(BF16), x[b, :, pl.ds(0, META)],
            (((1,), (1,)), ((), ())), preferred_element_type=F32,
        )
        owned = jnp.where(owner == p.astype(F32), 1.0, 0.0)
        rank = jnp.dot(owned.astype(BF16), before, preferred_element_type=F32)
        slot = lax.broadcasted_iota(jnp.int32, (SLOTS, rows_dev), 0).astype(F32)
        return jnp.where(rank == slot, owned, 0.0).astype(BF16)

    def choose(b):
        hit = selection(b)
        chosen[b] = hit
        tags[b] = jnp.dot(hit, x[b, :, pl.ds(0, META)], preferred_element_type=F32).astype(BF16)

    def pick(b, q):
        got = jnp.dot(chosen[b], x[b, :, piece(q)], preferred_element_type=F32).astype(BF16)

        @pl.when(q != me)
        def _():
            picked[b, q, :, pl.ds(0, META)] = tags[b]
            picked[b, q, :, pl.ds(META, part)] = got
            rcopy(picked.at[b, q], rows.at[b, me], rsend.at[b, q], rrecv.at[b, me], p, q).start()

        @pl.when(q == me)
        def _():
            rows[b, me, :, pl.ds(0, META)] = tags[b]
            rows[b, me, :, pl.ds(META, part)] = got

    def arrive(b, q):
        rcopy(
            x.at[b, :, sent(q)], x.at[b, :, sent(q)], hright.at[b, q], hrecv.at[b, q], p, peers[0]
        ).wait_recv()

        @pl.when(jnp.logical_and(b < p, p + 1 < pools))
        def _():
            to_right(b, q).start()

        @pl.when(jnp.logical_and(b > p, p >= 1))
        def _():
            to_left(b, q).start()

    def project(b, q):
        tile = tile_of(cols)
        for j in range(cols // tile):
            at = pl.ds(j * tile, tile)
            term = jnp.dot(
                x[b, :, piece(q)], w[pl.ds(q * part, part), at], preferred_element_type=F32
            )
            if q > 0:
                term = term + acc[b, :, at]
            if q == shards - 1:
                base[b, :, at] = term.astype(BF16)
            else:
                acc[b, :, at] = term

    mine_cols = pl.ds(pl.multiple_of(p * cols, 128), cols)
    mine_slots = pl.ds(pl.multiple_of(p * SLOTS, SLOTS), SLOTS)

    def base_copy(b):
        return rcopy(base.at[b], home_base.at[:, mine_cols], bsend.at[b], brecv.at[p], b, me)

    def delta_copy(b, sh):
        return rcopy(
            delta.at[b, sh], home_delta.at[me, mine_slots], dsend.at[b, sh], drecv.at[p, me], b, sh
        )

    lane = lax.broadcasted_iota(jnp.int32, (many, 256), 1) // ranks
    lower = lax.broadcasted_iota(jnp.int32, (many // 2, 128), 1) < 64

    def adapter_of(b):
        tag = rows[b, :, :, pl.ds(0, META)].reshape(many, META).astype(F32)
        return tag[:, 1:2].astype(jnp.int32)

    def shrink(b):
        for sh in peers:
            rcopy(rows.at[b, sh], rows.at[b, sh], rsend.at[b, sh], rrecv.at[b, sh], p, sh).wait_recv()
        adapter = adapter_of(b)
        here = rows[b, :, :, pl.ds(META, part)].reshape(many, part)
        total = jnp.zeros((many, 128), F32)
        for j in range(tiles):
            term = lax.dot_general(
                here, dn[pl.ds(j * 256, 256), :], (((1,), (1,)), ((), ())),
                preferred_element_type=F32,
            )
            term = jnp.where(lane + j * each == adapter, term, 0.0)
            total = total + term[:, :128] + term[:, 128:]
        total = total + pltpu.roll(total, 64, 1)
        packed = jnp.where(lower, total[: many // 2], total[many // 2 :])
        low_out[b] = packed
        low[b, me] = packed
        for sh in peers:
            rcopy(low_out.at[b], low.at[b, me], lsend.at[b, sh], lrecv.at[b, me], p, sh).start()

    def grow(b):
        for sh in peers:
            rcopy(low_out.at[b], low.at[b, sh], lsend.at[b, sh], lrecv.at[b, sh], p, sh).wait_recv()
        adapter = adapter_of(b)
        both = low[b, 0]
        for sh in range(1, shards):
            both = both + low[b, sh]
        both = both.astype(BF16).astype(F32)
        turned = pltpu.roll(both, 64, 1)
        full = jnp.concatenate(
            [jnp.where(lower, both, turned), jnp.where(lower, turned, both)], axis=0
        )
        full = jnp.concatenate([full, full], axis=1)
        spread = jnp.concatenate(
            [
                jnp.where(lane + j * each == adapter, full, 0.0).astype(BF16)
                for j in range(tiles)
            ],
            axis=1,
        )
        rest = jnp.dot(spread, up[:, pl.ds(3 * quarter, quarter)], preferred_element_type=F32)
        top = lax.broadcasted_iota(jnp.int32, (many, quarter), 0) % SLOTS < HELD
        for j in range(3):
            at = pl.ds(j * quarter, quarter)
            term = jnp.dot(spread, up[:, at], preferred_element_type=F32)
            term = jnp.where(top, term, pltpu.roll(rest, HELD - 4 * j, 0))
            delta[b, :, :, at] = (ADAPTER_SCALE * term).astype(BF16).reshape(shards, SLOTS, quarter)
        for sh in range(shards):
            @pl.when(jnp.logical_or(b != p, sh != me))
            def _():
                delta_copy(b, sh).start()

            @pl.when(jnp.logical_and(b == p, sh == me))
            def _():
                home_delta[me, mine_slots] = delta[b, sh]

    def both_sides(t, f):
        def turn(i, c):
            b = jnp.where(i == 0, p - t, p + t)
            inside = jnp.logical_and(b >= 0, b < pools)
            valid = jnp.logical_and(inside, jnp.logical_or(i == 0, t != 0))

            @pl.when(valid)
            def _():
                f(b)
            return c

        lax.fori_loop(0, 2, turn, 0)

    def step(t, carry):
        for q in range(shards):
            def take(b):
                @pl.when(b != p)
                def _():
                    arrive(b, q)
                if q == 0:
                    choose(b)
                pick(b, q)

            both_sides(t, take)
            if q == 1:
                @pl.when(t == 0)
                def _():
                    loads[0].wait()
            if q == 3:
                @pl.when(t == 0)
                def _():
                    loads[1].wait()
            if q > 0:
                both_sides(t, lambda b: project(b, q - 1))
            if q == 0:
                @pl.when(t == 1)
                def _():
                    loads[3].wait()

                @pl.when(t > 0)
                def _():
                    both_sides(t - 1, grow)

        @pl.when(t == 0)
        def _():
            loads[2].wait()
        both_sides(t, shrink)

        def finish(b):
            project(b, shards - 1)

            @pl.when(b != p)
            def _():
                base_copy(b).start()

            @pl.when(b == p)
            def _():
                home_base[:, mine_cols] = base[b]

        both_sides(t, finish)
        return carry

    lax.fori_loop(0, pools, step, 0)
    both_sides(pools - 1, grow)

    slots = pools * SLOTS
    lanes = lax.broadcasted_iota(jnp.int32, (rows_dev, slots), 1)
    owner = jnp.where(owner_column == lanes // SLOTS, 1.0, 0.0)
    after = jnp.where(down_axis > along, 1.0, 0.0).astype(BF16)
    rank = jnp.dot(after, owner.astype(BF16), preferred_element_type=F32)
    seat = lanes % SLOTS
    place = jnp.where(rank == seat.astype(F32), owner, 0.0).astype(BF16)
    tails = [
        jnp.where(
            jnp.logical_and(seat >= HELD, rank == (seat - HELD + 4 * k).astype(F32)), owner, 0.0
        ).astype(BF16)
        for k in range(3)
    ]

    places = jnp.concatenate([place] + tails, axis=0)

    def base_wait(z, carry):
        @pl.when(z != p)
        def _():
            dst = home_base.at[:, pl.ds(pl.multiple_of(z * cols, 128), cols)]
            rcopy(base.at[z], dst, bsend.at[z], brecv.at[z], z, me).wait_recv()
        return carry

    lax.fori_loop(0, pools, base_wait, 0)

    for sh in range(shards):
        def delta_wait(z, carry):
            @pl.when(jnp.logical_or(z != p, sh != me))
            def _():
                dst = home_delta.at[sh, pl.ds(pl.multiple_of(z * SLOTS, SLOTS), SLOTS)]
                rcopy(delta.at[z, sh], dst, dsend.at[z, sh], drecv.at[z, sh], z, sh).wait_recv()
            return carry

        lax.fori_loop(0, pools, delta_wait, 0)
        start = sh * part
        wide = 3 * quarter
        term = jnp.dot(places, home_delta[sh], preferred_element_type=F32)
        at = pl.ds(start, wide)
        out_ref[:, at] = (home_base[:, at].astype(F32) + term[:rows_dev]).astype(BF16)
        rest = term[rows_dev : 2 * rows_dev, :quarter]
        rest = rest + term[2 * rows_dev : 3 * rows_dev, quarter : 2 * quarter]
        rest = rest + term[3 * rows_dev :, 2 * quarter :]
        at = pl.ds(start + wide, quarter)
        out_ref[:, at] = (home_base[:, at].astype(F32) + rest).astype(BF16)

    def drain(b, carry):
        for q in range(shards):
            @pl.when(jnp.logical_and(b <= p, p + 1 < pools))
            def _():
                to_right(b, q).wait_send()

            @pl.when(jnp.logical_and(b >= p, p >= 1))
            def _():
                to_left(b, q).wait_send()

            @pl.when(q != me)
            def _():
                rcopy(picked.at[b, q], rows.at[b, me], rsend.at[b, q], rrecv.at[b, me], p, q).wait_send()
                rcopy(low_out.at[b], low.at[b, me], lsend.at[b, q], lrecv.at[b, me], p, q).wait_send()

            @pl.when(jnp.logical_or(b != p, q != me))
            def _():
                delta_copy(b, q).wait_send()

        @pl.when(b != p)
        def _():
            base_copy(b).wait_send()
        return carry

    lax.fori_loop(0, pools, drain, 0)


def local(hidden, query_weight_matrix, adapter_down_weight, adapter_up_weight, adapter_index_rows):
    pools = lax.axis_size("pool")
    chips = lax.axis_size("chip")
    shards = lax.axis_size("sub") * chips
    row_count, width = hidden.shape
    cols = query_weight_matrix.shape[1]
    stack, ranks, part = adapter_down_weight.shape
    if 2 + row_count // (pools - 1) > HELD:
        raise ValueError("owner overflow")
    dma = pltpu.SemaphoreType.DMA
    vmem = pl.BlockSpec(memory_space=pltpu.VMEM)
    hbm = pl.BlockSpec(memory_space=pl.ANY)
    return pl.pallas_call(
        functools.partial(kernel, pools, chips, shards, stack),
        out_shape=jax.ShapeDtypeStruct((row_count, width), BF16),
        in_specs=[hbm, vmem, hbm, hbm, hbm],
        out_specs=vmem,
        scratch_shapes=[
            pltpu.VMEM((pools, row_count, META + width), BF16),
            pltpu.VMEM((width, cols), BF16),
            pltpu.VMEM((stack * ranks, part), BF16),
            pltpu.VMEM((stack * ranks, part), BF16),
            pltpu.VMEM((pools, SLOTS, row_count), BF16),
            pltpu.VMEM((pools, SLOTS, META), BF16),
            pltpu.VMEM((pools, shards, SLOTS, META + part), BF16),
            pltpu.VMEM((pools, shards, SLOTS, META + part), BF16),
            pltpu.VMEM((pools, shards * SLOTS // 2, 128), F32),
            pltpu.VMEM((pools, shards, shards * SLOTS // 2, 128), F32),
            pltpu.VMEM((pools, shards, SLOTS, part - part // 4), BF16),
            pltpu.VMEM((shards, pools * SLOTS, part - part // 4), BF16),
            pltpu.VMEM((pools, row_count, cols), BF16),
            pltpu.VMEM((row_count, width), BF16),
            pltpu.VMEM((pools, row_count, cols), F32),
            dma((5,)),
            dma((pools, shards)),
            dma((pools, shards)),
            dma((pools, shards)),
            dma((pools, shards)),
            dma((pools, shards)),
            dma((pools, shards)),
            dma((pools, shards)),
            dma((pools,)),
            dma((pools,)),
            dma((pools, shards)),
            dma((pools, shards)),
        ],
        compiler_params=pltpu.CompilerParams(
            collective_id=0, has_side_effects=True, vmem_limit_bytes=56 * 1024 * 1024
        ),
    )(
        hidden,
        adapter_index_rows[None, :],
        query_weight_matrix,
        adapter_down_weight.reshape(stack * ranks, part),
        adapter_up_weight.reshape(stack * ranks, part),
    )


def solution(mesh):
    in_specs = (
        P(("groups", "pool", "sub", "chip"), None),
        P(None, "pool"),
        P("pool", None, ("sub", "chip")),
        P("pool", None, ("sub", "chip")),
        P(("groups", "pool", "sub", "chip")),
    )
    out_specs = P(("groups", "pool", "sub", "chip"), None)
    return jax.shard_map(local, mesh=mesh, in_specs=in_specs, out_specs=out_specs, check_vma=False)
```

```python
import functools

import jax
import jax.numpy as jnp
from jax import lax
from jax.experimental import pallas as pl
from jax.experimental.pallas import tpu as pltpu
from jax.sharding import PartitionSpec as P

ADAPTER_SCALE = 0.5
SLOTS = 16
HELD = 12
META = 128
MESH = pl.DeviceIdType.MESH
F32 = jnp.float32
BF16 = jnp.bfloat16


def tile_of(extent):
    return 256 if extent % 256 == 0 else extent


def kernel(
    pools, chips, shards, stack,
    h_hbm, idx_ref, w_hbm, dn_hbm, up_hbm, out_ref,
    x, w, dn, up, picked, rows, low_out, low, delta, home_delta, base, home_base, acc,
    wsem, hright, hleft, hrecv, rsend, rrecv, lsend, lrecv, bsend, brecv, dsend, drecv,
):
    p = lax.axis_index("pool")
    me = lax.axis_index("sub") * chips + lax.axis_index("chip")
    rows_dev, width = h_hbm.shape
    cols = w.shape[1]
    part = width // shards
    half = width // 2
    quarter = part // 4
    ranks = dn.shape[0] // stack
    tiles = stack * ranks // 256
    each = 256 // ranks
    many = shards * SLOTS

    def where_is(z, sh):
        return {"pool": z, "sub": sh // chips, "chip": sh % chips}

    def rcopy(src, dst, ssem, rsem, z, sh):
        return pltpu.make_async_remote_copy(
            src_ref=src, dst_ref=dst, send_sem=ssem, recv_sem=rsem,
            device_id=where_is(z, sh), device_id_type=MESH,
        )

    peers = [(me + d) % shards for d in range(1, shards)]

    barrier = pltpu.get_barrier_semaphore()

    def greet(z, sh):
        pl.semaphore_signal(barrier, inc=1, device_id=where_is(z, sh), device_id_type=MESH)

    @pl.when(p >= 1)
    def _():
        greet(p - 1, me)

    @pl.when(p + 1 < pools)
    def _():
        greet(p + 1, me)

    for sh in peers:
        greet(p, sh)

    loads = [
        pltpu.make_async_copy(w_hbm.at[pl.ds(0, half)], w.at[pl.ds(0, half)], wsem.at[0]),
        pltpu.make_async_copy(w_hbm.at[pl.ds(half, half)], w.at[pl.ds(half, half)], wsem.at[1]),
        pltpu.make_async_copy(dn_hbm, dn, wsem.at[2]),
        pltpu.make_async_copy(up_hbm, up, wsem.at[3]),
        pltpu.make_async_copy(h_hbm, x.at[p, :, pl.ds(META, width)], wsem.at[4]),
    ]
    for i in (4, 0, 2, 1, 3):
        loads[i].start()

    square = (rows_dev, rows_dev)
    down_axis = lax.broadcasted_iota(jnp.int32, square, 0)
    along = lax.broadcasted_iota(jnp.int32, square, 1)
    index = jnp.broadcast_to(idx_ref[...], square).astype(F32)
    column = jnp.sum(jnp.where(down_axis == along, index, 0.0), axis=1, keepdims=True)
    column = column.astype(jnp.int32)
    owner_column = column // stack
    first = lax.broadcasted_iota(jnp.int32, (rows_dev, META), 1) == 0
    meta = jnp.where(first, owner_column, column - owner_column * stack)
    x[p, :, pl.ds(0, META)] = meta.astype(F32).astype(BF16)

    greeters = jnp.minimum(p, 1) + jnp.minimum(pools - 1 - p, 1) + shards - 1
    pl.semaphore_wait(barrier, greeters)
    loads[4].wait()

    def piece(q):
        return pl.ds(META + q * part, part)

    def sent(q):
        return pl.ds(0, META + part) if q == 0 else piece(q)

    def to_right(b, q):
        ref = x.at[b, :, sent(q)]
        return rcopy(ref, ref, hright.at[b, q], hrecv.at[b, q], p + 1, me)

    def to_left(b, q):
        ref = x.at[b, :, sent(q)]
        return rcopy(ref, ref, hleft.at[b, q], hrecv.at[b, q], p - 1, me)

    for q in range(shards):
        @pl.when(p + 1 < pools)
        def _():
            to_right(p, q).start()

        @pl.when(p >= 1)
        def _():
            to_left(p, q).start()

    before = jnp.where(down_axis < along, 1.0, 0.0).astype(BF16)

    def selection(b):
        pick_owner = lax.broadcasted_iota(jnp.int32, (SLOTS, META), 1) == 0
        owner = lax.dot_general(
            jnp.where(pick_owner, 1.0, 0.0).astype(BF16), x[b, :, pl.ds(0, META)],
            (((1,), (1,)), ((), ())), preferred_element_type=F32,
        )
        owned = jnp.where(owner == p.astype(F32), 1.0, 0.0)
        rank = jnp.dot(owned.astype(BF16), before, preferred_element_type=F32)
        slot = lax.broadcasted_iota(jnp.int32, (SLOTS, rows_dev), 0).astype(F32)
        return jnp.where(rank == slot, owned, 0.0).astype(BF16)

    def pick(b, chosen, tag, q):
        got = jnp.dot(chosen, x[b, :, piece(q)], preferred_element_type=F32).astype(BF16)

        @pl.when(q != me)
        def _():
            picked[b, q, :, pl.ds(0, META)] = tag
            picked[b, q, :, pl.ds(META, part)] = got
            rcopy(picked.at[b, q], rows.at[b, me], rsend.at[b, q], rrecv.at[b, me], p, q).start()

        @pl.when(q == me)
        def _():
            rows[b, me, :, pl.ds(0, META)] = tag
            rows[b, me, :, pl.ds(META, part)] = got

    def select_tag(b):
        chosen = selection(b)
        tag = jnp.dot(chosen, x[b, :, pl.ds(0, META)], preferred_element_type=F32).astype(BF16)
        return chosen, tag

    def arrive(b, q, from_left):
        rcopy(
            x.at[b, :, sent(q)], x.at[b, :, sent(q)], hright.at[b, q], hrecv.at[b, q], p, peers[0]
        ).wait_recv()
        if from_left:
            @pl.when(p + 1 < pools)
            def _():
                to_right(b, q).start()
        else:
            @pl.when(p >= 1)
            def _():
                to_left(b, q).start()

    def receive(b, from_left):
        arrive(b, 0, from_left)
        chosen, tag = select_tag(b)
        pick(b, chosen, tag, 0)
        for q in range(1, shards):
            arrive(b, q, from_left)
            pick(b, chosen, tag, q)

    def project(b, k, last):
        tile = tile_of(cols)

        for j in range(cols // tile):
            at = pl.ds(j * tile, tile)
            term = jnp.dot(
                x[b, :, pl.ds(META + k * half, half)], w[pl.ds(k * half, half), at],
                preferred_element_type=F32,
            )
            if last:
                base[b, :, at] = (acc[b, :, at] + term).astype(BF16)
            else:
                acc[b, :, at] = term

    mine_cols = pl.ds(pl.multiple_of(p * cols, 128), cols)
    mine_slots = pl.ds(pl.multiple_of(p * SLOTS, SLOTS), SLOTS)

    def base_copy(b):
        return rcopy(base.at[b], home_base.at[:, mine_cols], bsend.at[b], brecv.at[p], b, me)

    def delta_copy(b, sh):
        return rcopy(
            delta.at[b, sh], home_delta.at[me, mine_slots], dsend.at[b, sh], drecv.at[p, me], b, sh
        )

    lane = lax.broadcasted_iota(jnp.int32, (many, 256), 1) // ranks
    lower = lax.broadcasted_iota(jnp.int32, (many // 2, 128), 1) < 64

    def adapter_of(b):
        tag = rows[b, :, :, pl.ds(0, META)].reshape(many, META).astype(F32)
        return tag[:, 1:2].astype(jnp.int32)

    def shrink(b):
        for sh in peers:
            rcopy(rows.at[b, sh], rows.at[b, sh], rsend.at[b, sh], rrecv.at[b, sh], p, sh).wait_recv()
        adapter = adapter_of(b)
        here = rows[b, :, :, pl.ds(META, part)].reshape(many, part)
        total = jnp.zeros((many, 128), F32)
        for j in range(tiles):
            term = lax.dot_general(
                here, dn[pl.ds(j * 256, 256), :], (((1,), (1,)), ((), ())),
                preferred_element_type=F32,
            )
            term = jnp.where(lane + j * each == adapter, term, 0.0)
            total = total + term[:, :128] + term[:, 128:]
        total = total + pltpu.roll(total, 64, 1)
        packed = jnp.where(lower, total[: many // 2], total[many // 2 :])
        low_out[b] = packed
        low[b, me] = packed
        for sh in peers:
            rcopy(low_out.at[b], low.at[b, me], lsend.at[b, sh], lrecv.at[b, me], p, sh).start()

    def grow(b):
        for sh in peers:
            rcopy(low_out.at[b], low.at[b, sh], lsend.at[b, sh], lrecv.at[b, sh], p, sh).wait_recv()
        adapter = adapter_of(b)
        both = low[b, 0]
        for sh in range(1, shards):
            both = both + low[b, sh]
        both = both.astype(BF16).astype(F32)
        turned = pltpu.roll(both, 64, 1)
        full = jnp.concatenate(
            [jnp.where(lower, both, turned), jnp.where(lower, turned, both)], axis=0
        )
        full = jnp.concatenate([full, full], axis=1)
        spread = jnp.concatenate(
            [
                jnp.where(lane + j * each == adapter, full, 0.0).astype(BF16)
                for j in range(tiles)
            ],
            axis=1,
        )
        rest = jnp.dot(spread, up[:, pl.ds(3 * quarter, quarter)], preferred_element_type=F32)
        top = lax.broadcasted_iota(jnp.int32, (many, quarter), 0) % SLOTS < HELD
        for j in range(3):
            at = pl.ds(j * quarter, quarter)
            term = jnp.dot(spread, up[:, at], preferred_element_type=F32)
            term = jnp.where(top, term, pltpu.roll(rest, HELD - 4 * j, 0))
            delta[b, :, :, at] = (ADAPTER_SCALE * term).astype(BF16).reshape(shards, SLOTS, quarter)
        for sh in range(shards):
            @pl.when(jnp.logical_or(b != p, sh != me))
            def _():
                delta_copy(b, sh).start()

            @pl.when(jnp.logical_and(b == p, sh == me))
            def _():
                home_delta[me, mine_slots] = delta[b, sh]

    def both_sides(t, f):
        def turn(i, c):
            b = jnp.where(i == 0, p - t, p + t)
            valid = jnp.logical_and(jnp.logical_and(b >= 0, b < pools), jnp.logical_or(i == 0, t > 0))

            @pl.when(valid)
            def _():
                f(b)
            return c

        lax.fori_loop(0, 2, turn, 0)

    chosen, tag = select_tag(p)
    for q in range(shards):
        pick(p, chosen, tag, q)

    def step(t, carry):
        @pl.when(t == 0)
        def _():
            loads[0].wait()
        both_sides(t, lambda b: project(b, 0, False))

        @pl.when(t == 0)
        def _():
            loads[2].wait()
        both_sides(t, shrink)

        @pl.when(t == 0)
        def _():
            loads[1].wait()

        def finish(b):
            project(b, 1, True)

            @pl.when(b != p)
            def _():
                base_copy(b).start()

            @pl.when(b == p)
            def _():
                home_base[:, mine_cols] = base[b]

        inner = jnp.logical_and(jnp.logical_and(p - t >= 0, p + t < pools), t > 0)

        def phase(i, c):
            @pl.when(i == jnp.where(inner, 1, 0))
            def _():
                both_sides(t, finish)

            @pl.when(i == jnp.where(inner, 0, 1))
            def _():
                @pl.when(p - 1 - t >= 0)
                def _():
                    receive(p - 1 - t, True)

                @pl.when(p + 1 + t < pools)
                def _():
                    receive(p + 1 + t, False)
            return c

        lax.fori_loop(0, 2, phase, 0)

        @pl.when(t == 0)
        def _():
            loads[3].wait()
        both_sides(t, grow)
        return carry

    lax.fori_loop(0, pools, step, 0)

    slots = pools * SLOTS
    lanes = lax.broadcasted_iota(jnp.int32, (rows_dev, slots), 1)
    owner = jnp.where(owner_column == lanes // SLOTS, 1.0, 0.0)
    after = jnp.where(down_axis > along, 1.0, 0.0).astype(BF16)
    rank = jnp.dot(after, owner.astype(BF16), preferred_element_type=F32)
    seat = lanes % SLOTS
    place = jnp.where(rank == seat.astype(F32), owner, 0.0).astype(BF16)
    tails = [
        jnp.where(
            jnp.logical_and(seat >= HELD, rank == (seat - HELD + 4 * k).astype(F32)), owner, 0.0
        ).astype(BF16)
        for k in range(3)
    ]

    places = jnp.concatenate([place] + tails, axis=0)

    def base_wait(z, carry):
        @pl.when(z != p)
        def _():
            dst = home_base.at[:, pl.ds(pl.multiple_of(z * cols, 128), cols)]
            rcopy(base.at[z], dst, bsend.at[z], brecv.at[z], z, me).wait_recv()
        return carry

    lax.fori_loop(0, pools, base_wait, 0)

    for sh in range(shards):
        def delta_wait(z, carry):
            @pl.when(jnp.logical_or(z != p, sh != me))
            def _():
                dst = home_delta.at[sh, pl.ds(pl.multiple_of(z * SLOTS, SLOTS), SLOTS)]
                rcopy(delta.at[z, sh], dst, dsend.at[z, sh], drecv.at[z, sh], z, sh).wait_recv()
            return carry

        lax.fori_loop(0, pools, delta_wait, 0)
        start = sh * part
        wide = 3 * quarter
        term = jnp.dot(places, home_delta[sh], preferred_element_type=F32)
        at = pl.ds(start, wide)
        out_ref[:, at] = (home_base[:, at].astype(F32) + term[:rows_dev]).astype(BF16)
        rest = term[rows_dev : 2 * rows_dev, :quarter]
        rest = rest + term[2 * rows_dev : 3 * rows_dev, quarter : 2 * quarter]
        rest = rest + term[3 * rows_dev :, 2 * quarter :]
        at = pl.ds(start + wide, quarter)
        out_ref[:, at] = (home_base[:, at].astype(F32) + rest).astype(BF16)

    def drain(b, carry):
        for q in range(shards):
            @pl.when(jnp.logical_and(b <= p, p + 1 < pools))
            def _():
                to_right(b, q).wait_send()

            @pl.when(jnp.logical_and(b >= p, p >= 1))
            def _():
                to_left(b, q).wait_send()

            @pl.when(q != me)
            def _():
                rcopy(picked.at[b, q], rows.at[b, me], rsend.at[b, q], rrecv.at[b, me], p, q).wait_send()
                rcopy(low_out.at[b], low.at[b, me], lsend.at[b, q], lrecv.at[b, me], p, q).wait_send()

            @pl.when(jnp.logical_or(b != p, q != me))
            def _():
                delta_copy(b, q).wait_send()

        @pl.when(b != p)
        def _():
            base_copy(b).wait_send()
        return carry

    lax.fori_loop(0, pools, drain, 0)


def local(hidden, query_weight_matrix, adapter_down_weight, adapter_up_weight, adapter_index_rows):
    pools = lax.axis_size("pool")
    chips = lax.axis_size("chip")
    shards = lax.axis_size("sub") * chips
    row_count, width = hidden.shape
    cols = query_weight_matrix.shape[1]
    stack, ranks, part = adapter_down_weight.shape
    if 2 + row_count // (pools - 1) > HELD:
        raise ValueError("owner overflow")
    dma = pltpu.SemaphoreType.DMA
    vmem = pl.BlockSpec(memory_space=pltpu.VMEM)
    hbm = pl.BlockSpec(memory_space=pl.ANY)
    return pl.pallas_call(
        functools.partial(kernel, pools, chips, shards, stack),
        out_shape=jax.ShapeDtypeStruct((row_count, width), BF16),
        in_specs=[hbm, vmem, hbm, hbm, hbm],
        out_specs=vmem,
        scratch_shapes=[
            pltpu.VMEM((pools, row_count, META + width), BF16),
            pltpu.VMEM((width, cols), BF16),
            pltpu.VMEM((stack * ranks, part), BF16),
            pltpu.VMEM((stack * ranks, part), BF16),
            pltpu.VMEM((pools, shards, SLOTS, META + part), BF16),
            pltpu.VMEM((pools, shards, SLOTS, META + part), BF16),
            pltpu.VMEM((pools, shards * SLOTS // 2, 128), F32),
            pltpu.VMEM((pools, shards, shards * SLOTS // 2, 128), F32),
            pltpu.VMEM((pools, shards, SLOTS, part - part // 4), BF16),
            pltpu.VMEM((shards, pools * SLOTS, part - part // 4), BF16),
            pltpu.VMEM((pools, row_count, cols), BF16),
            pltpu.VMEM((row_count, width), BF16),
            pltpu.VMEM((pools, row_count, cols), F32),
            dma((5,)),
            dma((pools, shards)),
            dma((pools, shards)),
            dma((pools, shards)),
            dma((pools, shards)),
            dma((pools, shards)),
            dma((pools, shards)),
            dma((pools, shards)),
            dma((pools,)),
            dma((pools,)),
            dma((pools, shards)),
            dma((pools, shards)),
        ],
        compiler_params=pltpu.CompilerParams(
            collective_id=0, has_side_effects=True, vmem_limit_bytes=56 * 1024 * 1024
        ),
    )(
        hidden,
        adapter_index_rows[None, :],
        query_weight_matrix,
        adapter_down_weight.reshape(stack * ranks, part),
        adapter_up_weight.reshape(stack * ranks, part),
    )


def solution(mesh):
    in_specs = (
        P(("groups", "pool", "sub", "chip"), None),
        P(None, "pool"),
        P("pool", None, ("sub", "chip")),
        P("pool", None, ("sub", "chip")),
        P(("groups", "pool", "sub", "chip")),
    )
    out_specs = P(("groups", "pool", "sub", "chip"), None)
    return jax.shard_map(local, mesh=mesh, in_specs=in_specs, out_specs=out_specs, check_vma=False)
```
